32 devices in a mesh: groups: 2 (over y), ctx: 4 (over z), head: 2 (over x), sub: 2 (over core).
Axes of the slice: x: 2, y: 2, z: 4, core: 2. Of those that a mesh axis runs over, the one named last changes fastest.
Arguments:
- query_rows: bfloat16 [128, 128, 1024], P(('groups', 'ctx', 'sub'), 'head'), parts along dimension 0, may hold values from -16 to 16
- key_rows: bfloat16 [128, 128, 1024], P(('groups', 'ctx', 'sub'), 'head'), parts along dimension 0, may hold values from -6 to 6
- value_rows: bfloat16 [128, 128, 1024], P(('groups', 'ctx', 'sub'), 'head'), parts along dimension 0, may hold values from -4 to 4
- cotangent: bfloat16 [128, 128, 1024], P(('groups', 'ctx', 'sub'), 'head'), parts along dimension 0, may hold values from -4 to 4
- neighbours: int32 [128, 16], P('groups'), parts along dimension 0, may hold values from -1 to 63, as said below
- valid_counts: int32 [128], P('groups'), parts along dimension 0, may hold values from 32 to 128
Outputs:
- attended: bfloat16 [128, 128, 1024], P(('groups', 'ctx', 'sub'), 'head'), parts along dimension 0
- query_grad: bfloat16 [128, 128, 1024], P(('groups', 'ctx', 'sub'), 'head'), parts along dimension 0
- key_grad: bfloat16 [128, 128, 1024], P(('groups', 'ctx', 'sub'), 'head'), parts along dimension 0
- value_grad: bfloat16 [128, 128, 1024], P(('groups', 'ctx', 'sub'), 'head'), parts along dimension 0
The draws below stay inside these ranges and needn't reach their ends.
There are 2 independent parts, one for each index of `groups`. The reference program is written for one: setup_inputs(seed, part) draws one part's arguments, and reference() takes and returns one part's arrays. A program takes and returns all parts, laid end to end along the dimension named above; each array names one. Nothing has to cross between parts.
Inputs may be any that keep to these rules, and one draw needn't show every extreme that they name: `neighbours`: row b begins with b itself; its other entries are distinct blocks at most 8 blocks away from b, or -1 for an empty slot; a block with 8 blocks on both sides has no empty slot.
All inputs are finite; a program needn't handle non-finite values.
Results may differ from the reference program's by a relative error of at most 0.012.
Values may be sent and summed in bfloat16 or wider, within the bound.
No kernel may reach another device: no remote copies, remote signals or barrier semaphores. Data moves between devices by JAX's collectives and lax.ppermute only.
A program may use at most 128 MiB of HBM per device.

```python
import jax
import jax.numpy as jnp
from jax import lax

DH = 128
BQ = 128
NBR = 16
WIN = 8
D = 1024
NBLK = 64


def paired_rows(key):
    base_key = jax.random.fold_in(key, 11)
    first_key, second_key = jax.random.split(base_key, 2)
    full_shape = (NBLK, BQ, D)
    query_draw = jnp.clip(jax.random.normal(first_key, full_shape, jnp.float32), -4.0, 4.0)
    keyset = jnp.clip(jax.random.normal(second_key, full_shape, jnp.float32), -4.0, 4.0)
    return (query_draw, keyset)


def draw_query_rows(key, part):
    return paired_rows(key)[0].astype(jnp.bfloat16)


def draw_key_rows(key, part):
    return paired_rows(key)[1].astype(jnp.bfloat16)


def draw_neighbours(key, part):
    blocks = jnp.arange(NBLK, dtype=jnp.int32)
    offsets = jnp.concatenate([jnp.arange(-WIN, 0, dtype=jnp.int32), jnp.arange(1, WIN + 1, dtype=jnp.int32)])
    candidate = blocks[:, None] + offsets[None, :]
    inside = (candidate >= 0) & (candidate < NBLK)
    noise = jax.random.randint(jax.random.fold_in(key, 5), (NBLK, 2 * WIN), 0, 1 << 20)
    column = jnp.arange(2 * WIN, dtype=jnp.int32)[None, :]
    ranking = jnp.where(inside, noise * 64 + column, -1 - column)
    unused, picked = lax.top_k(ranking, NBR - 1)
    chosen = jnp.take_along_axis(candidate, picked, axis=1)
    chosen_inside = jnp.take_along_axis(inside, picked, axis=1)
    chosen = jnp.where(chosen_inside, chosen, -1)
    return jnp.concatenate([blocks[:, None], chosen], axis=1).astype(jnp.int32)


def place_ends(values, stream_key, least, high):
    spot = [jax.random.randint(jax.random.fold_in(stream_key, axis), (), 0, length) for axis, length in enumerate(values.shape)]
    main_axis = values.shape.index(max(values.shape))
    next_to = spot[:main_axis] + [(spot[main_axis] + 1) % values.shape[main_axis]] + spot[main_axis + 1:]
    return values.at[tuple(spot)].set(least).at[tuple(next_to)].set(high)


def block_levels(stream_key, dims, shards, least, high):
    gain, own = 1.0, jax.random.fold_in(stream_key, 6)
    for dim, shards_of in shards:
        heights = jnp.exp(jax.random.uniform(jax.random.fold_in(own, dim), (shards_of,), jnp.float32, least / len(shards), high / len(shards)))
        gain = gain * jnp.repeat(heights, dims[dim] // shards_of).reshape([-1 if axis == dim else 1 for axis in range(len(dims))])
    return gain


def normal_values(key, shape, deviation, bound, shards=(), kind=jnp.bfloat16):
    values = deviation * jax.random.normal(key, shape, jnp.float32)
    if shards:
        values = values * block_levels(key, shape, shards, -0.22, 0.18)
    return jnp.clip(values, -bound, bound).astype(kind)


def setup_inputs(seed: int = 0, part: int = 0) -> dict:
    splits = jax.random.split(jax.random.key(seed), 7)
    part_keys = jax.random.split(jax.random.fold_in(splits[6], part), 7)
    query_rows = draw_query_rows(jax.random.fold_in(jax.random.fold_in(splits[6], part), 71), part)
    key_rows = draw_key_rows(jax.random.fold_in(jax.random.fold_in(splits[6], part), 71), part)
    value_rows = normal_values(part_keys[2], (NBLK, BQ, D), 1.0, 4.0, ((0, 8), (1, 2)))
    cotangent = normal_values(part_keys[3], (NBLK, BQ, D), 1.0, 4.0, ((0, 8), (1, 2)))
    neighbours = draw_neighbours(jax.random.fold_in(jax.random.fold_in(splits[6], part), 71), part)
    valid_counts = place_ends(jax.random.randint(part_keys[5], (NBLK,), BQ // 4, BQ + 1), jax.random.fold_in(part_keys[5], 1), BQ // 4, BQ).astype(jnp.int32)
    return dict(query_rows=query_rows, key_rows=key_rows, value_rows=value_rows, cotangent=cotangent, neighbours=neighbours, valid_counts=valid_counts)


NEGATIVE = -1.0e30


def split_heads(tile_rows):
    return tile_rows.reshape(tile_rows.shape[0], tile_rows.shape[1] // DH, DH).astype(jnp.float32)


def rounded(values_in):
    return lax.optimization_barrier(values_in.astype(jnp.bfloat16)).astype(jnp.float32)


def lookup(count_table, wanted):
    matches = wanted[..., None] == jnp.arange(count_table.shape[0], dtype=jnp.int32)
    return jnp.sum(jnp.where(matches, count_table, 0), axis=-1).astype(jnp.int32)


def key_mask(block_lists, count_table):
    key_count = jnp.where(block_lists >= 0, lookup(count_table, block_lists), 0)
    positions = jnp.arange(BQ, dtype=jnp.int32)
    return (positions[None, None, :] < key_count[..., None]).reshape(block_lists.shape[0], -1)


def scores(query_block, key_block, usable_block):
    raw_scores = jnp.einsum("qhd,khd->hqk", split_heads(query_block), split_heads(key_block))
    return jnp.where(usable_block[None, None, :], raw_scores * (DH ** -0.5), NEGATIVE)


def attend(query_block, key_block, value_block, usable_block, rows_ok):
    logits = scores(query_block, key_block, usable_block)
    highest = jnp.max(logits, axis=-1, keepdims=True)
    log_total = highest[..., 0] + jnp.log(jnp.sum(jnp.exp(logits - highest), axis=-1))
    probability = rounded(jnp.exp(logits - log_total[..., None]))
    mixture = jnp.einsum("hqk,khd->qhd", probability, split_heads(value_block))
    mixture = jnp.where(rows_ok[:, None, None], mixture, 0.0)
    return mixture.reshape(query_block.shape).astype(jnp.bfloat16), log_total


def key_terms(query_block, key_block, value_block, grad_block, log_block, delta_block, usable_block):
    probability = jnp.exp(scores(query_block, key_block, usable_block) - log_block[..., None])
    prob_grad = jnp.einsum("qhd,khd->hqk", split_heads(grad_block), split_heads(value_block))
    score_grad = rounded(probability * (prob_grad - delta_block[..., None]))
    key_part = jnp.einsum("hqk,qhd->khd", score_grad, split_heads(query_block)) * (DH ** -0.5)
    value_part = jnp.einsum("hqk,qhd->khd", rounded(probability), split_heads(grad_block))
    return score_grad, key_part.reshape(key_block.shape), value_part.reshape(key_block.shape)


def reference(query_rows, key_rows, value_rows, cotangent, neighbours, valid_counts):
    total_blocks = query_rows.shape[0]
    feature_width = query_rows.shape[2]
    positions = jnp.arange(BQ, dtype=jnp.int32)
    valid_rows = positions[None, :] < valid_counts[:, None]
    slot_index = jnp.clip(neighbours, 0, total_blocks - 1).astype(jnp.int32)
    usable = key_mask(neighbours, valid_counts)

    def forward_block(inputs):
        query_block, slot_block, usable_block, rows_ok = inputs
        key_block = key_rows[slot_block].reshape(-1, feature_width)
        value_block = value_rows[slot_block].reshape(-1, feature_width)
        return attend(query_block, key_block, value_block, usable_block, rows_ok)

    attended, log_total = lax.map(forward_block, (query_rows, slot_index, usable, valid_rows))
    grad_masked = jnp.where(valid_rows[:, :, None], cotangent, jnp.zeros_like(cotangent))
    heads_here = feature_width // DH
    attended_kept = lax.optimization_barrier(attended).astype(jnp.float32)
    row_delta = jnp.einsum("bqhd,bqhd->bhq", grad_masked.astype(jnp.float32).reshape(total_blocks, BQ, heads_here, DH), attended_kept.reshape(total_blocks, BQ, heads_here, DH))

    def backward_block(running, inputs):
        key_sum, value_sum = running
        query_block, grad_block, log_block, delta_block, slot_block, usable_block = inputs
        key_block = key_rows[slot_block].reshape(-1, feature_width)
        value_block = value_rows[slot_block].reshape(-1, feature_width)
        score_grad, key_part, value_part = key_terms(query_block, key_block, value_block, grad_block, log_block, delta_block, usable_block)
        query_part = jnp.einsum("hqk,khd->qhd", score_grad, split_heads(key_block)) * (DH ** -0.5)
        key_sum = key_sum.at[slot_block].add(key_part.reshape(-1, BQ, feature_width))
        value_sum = value_sum.at[slot_block].add(value_part.reshape(-1, BQ, feature_width))
        return (key_sum, value_sum), query_part.reshape(query_block.shape).astype(jnp.bfloat16)

    zeros_full = jnp.zeros((total_blocks, BQ, feature_width), jnp.float32)
    (key_sum, value_sum), query_grad = lax.scan(backward_block, (zeros_full, zeros_full), (query_rows, grad_masked, log_total, row_delta, slot_index, usable))
    return attended, query_grad, key_sum.astype(jnp.bfloat16), value_sum.astype(jnp.bfloat16)
```

```python
import functools

import jax
import jax.numpy as jnp
from jax import lax
from jax.experimental import pallas as pl
from jax.experimental.pallas import tpu as pltpu
from jax.sharding import PartitionSpec as P

DH = 128
BQ = 128
SCALE = DH ** (-0.5)
LOG2E = 1.4426950408889634
NEGATIVE = -1e30
ROW = ("ctx", "sub")


def group_sizes(count):
    return (1, count - 2, 1) if count > 2 else (1,) * count


def exchange(array, axis, by):
    size = lax.axis_size(axis)
    return lax.ppermute(array, axis, [((i + by) % size, i) for i in range(size)])


def near(array, first):
    size = lax.axis_size(ROW)
    pairs = []
    for i in range(first, size - 1, 2):
        pairs += [(i, i + 1), (i + 1, i)]
    return lax.ppermute(array, ROW, pairs)


def attend_kernel(meta, *refs, blocks, slots, parts, rows, aliased):
    (k_own, v_own, q_own, g_own, x_in, a_own, b_own, a_in, b_in) = refs[:9]
    refs = refs[9 + aliased :]
    (att_out, dq_out, y_out, kept_out, a_out, b_out) = refs[:6]
    (kv, kt, vt, bias, bd, bd2, sp, pd, acc) = refs[6:]
    here = meta[0]
    wide = 3 * blocks
    slot_at = 2
    own_at = slot_at + blocks * slots
    wide_at = own_at + blocks

    def start(s):
        return pl.multiple_of(lax.rem(here + s, parts) * rows, rows)

    for s in range(parts):
        at = pl.ds(start(s), rows)
        for t, own in ((0, k_own), (1, v_own)):
            lanes = slice(t * DH, (t + 1) * DH)
            kv[0:blocks, at, lanes] = own[...] if s == 0 else x_in[s - 1, t]
            kv[blocks : 2 * blocks, at, lanes] = a_own[t] if s == 0 else a_in[s - 1, t]
            kv[2 * blocks : wide, at, lanes] = b_own[t] if s == 0 else b_in[s - 1, t]
    kv[wide] = jnp.zeros((BQ, 2 * DH), jnp.bfloat16)
    bd[...] = jnp.zeros_like(bd)
    bd2[...] = jnp.zeros_like(bd2)
    acc[...] = jnp.zeros_like(acc)
    key_row = lax.broadcasted_iota(jnp.int32, (BQ, DH), 0)

    def prepare(w, carry):
        kt[w] = kv[w, :, 0:DH].T
        vt[w] = kv[w, :, DH : 2 * DH].T
        bias[w] = jnp.where(key_row < meta[wide_at + w], 0.0, NEGATIVE)
        return carry

    lax.fori_loop(0, wide + 1, prepare, 0)
    row = lax.broadcasted_iota(jnp.int32, (rows, DH), 0)

    def block(b, carry):
        count = meta[own_at + b]
        index = [meta[slot_at + b * slots + j] for j in range(slots)]
        for s in range(parts):
            at = start(s)
            q_part = q_own[b] if s == 0 else x_in[s - 1, 2, b]
            g_part = g_own[b] if s == 0 else x_in[s - 1, 3, b]
            g_part = jnp.where(row + at < count, g_part, jnp.zeros_like(g_part))
            low, high = pl.ds(at, rows), pl.ds(BQ + at, rows)
            bd[low, 0:DH] = q_part
            bd[high, DH : 2 * DH] = g_part
            bd2[low, 0:DH] = g_part
            bd2[high, DH : 2 * DH] = q_part
        keys = jnp.concatenate([kv[i] for i in index], axis=0)
        sp[...] = lax.dot_general(
            keys, bd[...], (((1,), (1,)), ((), ())), preferred_element_type=jnp.float32
        )
        top = None
        for j in range(slots):
            at = slice(j * BQ, (j + 1) * BQ)
            s = sp[at, 0:DH] + bias[index[j]]
            sp[at, 0:DH] = s
            high = jnp.max(s, axis=0, keepdims=True)
            top = high if top is None else jnp.maximum(top, high)
        shift = top * (SCALE * LOG2E)
        total = jnp.zeros((8, DH), jnp.float32)
        for j in range(slots):
            at = slice(j * BQ, (j + 1) * BQ)
            p = jnp.exp2(sp[at, 0:DH] * (SCALE * LOG2E) - shift)
            sp[at, 0:DH] = p
            total = total + jnp.sum(p.reshape(BQ // 8, 8, DH), axis=0)
        inverse = 1.0 / jnp.sum(total, axis=0, keepdims=True)
        for j in range(slots):
            at = slice(j * BQ, (j + 1) * BQ)
            p = sp[at, 0:DH] * inverse
            sp[at, 0:DH] = p
            pd[at, 0:DH] = p.astype(jnp.bfloat16)
        values_t = jnp.concatenate([vt[i] for i in index], axis=1)
        mixed = jnp.dot(values_t, pd[:, 0:DH], preferred_element_type=jnp.float32)
        lane = lax.broadcasted_iota(jnp.int32, (DH, BQ), 1)
        mixed = jnp.where(lane < count, mixed, 0.0).astype(jnp.bfloat16)
        grad_t = bd2[0:BQ, 0:DH].T.astype(jnp.float32)
        delta = jnp.sum(grad_t * mixed.astype(jnp.float32), axis=0, keepdims=True)
        for j in range(slots):
            at = slice(j * BQ, (j + 1) * BQ)
            d = sp[at, 0:DH] * (sp[at, DH : 2 * DH] - delta)
            pd[at, DH : 2 * DH] = d.astype(jnp.bfloat16)
        keys_t = jnp.concatenate([kt[i] for i in index], axis=1)
        turned = jnp.dot(keys_t, pd[:, DH : 2 * DH], preferred_element_type=jnp.float32)
        both = jnp.dot(pd[...], bd2[...], preferred_element_type=jnp.float32)
        for j in range(slots):
            acc[index[j]] += both[j * BQ : (j + 1) * BQ]
        bd2[0:BQ, DH : 2 * DH] = mixed.T
        bd2[BQ : 2 * BQ, 0:DH] = (turned * SCALE).T.astype(jnp.bfloat16)
        for s in range(parts):
            at = start(s)
            att_rows = bd2[pl.ds(at, rows), DH : 2 * DH]
            dq_rows = bd2[pl.ds(BQ + at, rows), 0:DH]
            if s == 0:
                att_out[b] = att_rows
                dq_out[b] = dq_rows
            else:
                y_out[s - 1, 0, b] = att_rows
                y_out[s - 1, 1, b] = dq_rows
        bd2[0:BQ, DH : 2 * DH] = jnp.zeros((BQ, DH), jnp.bfloat16)
        bd2[BQ : 2 * BQ, 0:DH] = jnp.zeros((BQ, DH), jnp.bfloat16)
        return carry

    lax.fori_loop(0, blocks, block, 0)
    for out, first in ((kept_out, 0), (a_out, blocks), (b_out, 2 * blocks)):
        out[:, :, 0:DH] = acc[first : first + blocks, :, 0:DH].astype(out.dtype)
        out[:, :, DH : 2 * DH] = (acc[first : first + blocks, :, DH : 2 * DH] * SCALE).astype(out.dtype)


def combine_kernel(meta, kept, a_in, b_in, *refs, blocks, parts, rows, aliased):
    dk_out, dv_out, y_out = refs[aliased : aliased + 3]
    total = refs[aliased + 3]
    here = meta[0]
    total[...] = (
        kept[...] + a_in[...].astype(jnp.float32) + b_in[...].astype(jnp.float32)
    ).astype(jnp.bfloat16)
    for s in range(parts):
        at = pl.ds(pl.multiple_of(lax.rem(here + s, parts) * rows, rows), rows)
        if s == 0:
            dv_out[...] = total[:, at, 0:DH]
            dk_out[...] = total[:, at, DH : 2 * DH]
        else:
            y_out[s - 1, 0] = total[:, at, DH : 2 * DH]
            y_out[s - 1, 1] = total[:, at, 0:DH]


def params(limit=None):
    return pltpu.CompilerParams(dimension_semantics=("arbitrary",), vmem_limit_bytes=limit)


def shards(query_rows, key_rows, value_rows, cotangent, neighbours, valid_counts):
    parts = lax.axis_size("head")
    here = lax.axis_index("head")
    blocks, rows, width = query_rows.shape
    slots = neighbours.shape[1]
    heads = width // DH // parts
    position = lax.axis_index(ROW)
    first_block = position * blocks
    odd = position % 2
    own_lists = lax.dynamic_slice_in_dim(neighbours, first_block, blocks, 0)
    own_counts = lax.dynamic_slice_in_dim(valid_counts, first_block, blocks, 0)
    offset = own_lists - first_block
    left_base = jnp.where(odd == 1, blocks, 2 * blocks)
    right_base = jnp.where(odd == 1, 2 * blocks, blocks)
    wide_index = jnp.where(
        offset < 0,
        left_base + offset + blocks,
        jnp.where(offset < blocks, offset, right_base + offset - blocks),
    )
    wide_index = jnp.where(own_lists < 0, 3 * blocks, wide_index)
    padded = jnp.pad(valid_counts, (blocks, blocks))
    wide_counts = lax.dynamic_slice_in_dim(padded, first_block, 3 * blocks, 0)
    left, middle, right = wide_counts[:blocks], wide_counts[blocks : 2 * blocks], wide_counts[2 * blocks :]
    first = jnp.where(odd == 1, left, right)
    second = jnp.where(odd == 1, right, left)
    zero = jnp.zeros((1,), jnp.int32)

    def meta_for(lane_block):
        return jnp.concatenate(
            [
                here[None],
                lane_block[None],
                wide_index.reshape(-1),
                own_counts,
                middle,
                first,
                second,
                zero,
            ]
        ).astype(jnp.int32)

    tensors = (key_rows, value_rows, query_rows, cotangent)
    sizes = group_sizes(heads)
    starts = [sum(sizes[:i]) for i in range(len(sizes))]

    def lanes_of(array, c, h, who):
        return lax.dynamic_slice_in_dim(array, (parts * c + who * h) * DH, h * DH, 2)

    received = []
    for c, h in zip(starts, sizes):
        pieces = []
        for s in range(1, parts):
            to = (here + parts - s) % parts
            pieces.append(exchange(jnp.stack([lanes_of(t, c, h, to) for t in tensors]), "head", s))
        received.append(jnp.stack(pieces) if len(pieces) > 1 else pieces[0][None])
    own = jnp.stack(
        [
            jnp.concatenate([lanes_of(t, c, h, here) for c, h in zip(starts, sizes)], axis=2)
            for t in (key_rows, value_rows)
        ]
    )
    a_own, b_own = near(own, 0), near(own, 1)

    bf16, f32 = jnp.bfloat16, jnp.float32
    whole = jax.ShapeDtypeStruct((blocks, rows, width), bf16)
    outs = {}
    sends = []
    for c, h, x_in in zip(starts, sizes, received):
        a_in, b_in = near(x_in[:, :2], 0), near(x_in[:, :2], 1)
        meta = meta_for(parts * c + here * h)
        own_spec = pl.BlockSpec((blocks, rows, DH), lambda i, m: (0, 0, m[1] + i))
        wide_spec = pl.BlockSpec((blocks, BQ, 2 * DH), lambda i, m: (0, 0, i))

        def piece_spec(n):
            return pl.BlockSpec((parts - 1, n, blocks, rows, DH), lambda i, m: (0, 0, 0, 0, i))

        halo_spec = pl.BlockSpec((2, blocks, rows, DH), lambda i, m, c=c: (0, 0, 0, c + i))
        any_spec = pl.BlockSpec(memory_space=pl.ANY)
        carried = [outs["att"], outs["dq"]] if outs else []
        aliased = len(carried)
        keys = slots * BQ
        att, dq, y_att, kept, a_grad, b_grad = pl.pallas_call(
            functools.partial(
                attend_kernel, blocks=blocks, slots=slots, parts=parts, rows=rows, aliased=aliased
            ),
            grid_spec=pltpu.PrefetchScalarGridSpec(
                num_scalar_prefetch=1,
                grid=(h,),
                in_specs=[own_spec] * 4
                + [piece_spec(4), halo_spec, halo_spec, piece_spec(2), piece_spec(2)]
                + [any_spec] * aliased,
                out_specs=[own_spec, own_spec, piece_spec(2), wide_spec, wide_spec, wide_spec],
                scratch_shapes=[
                    pltpu.VMEM((3 * blocks + 1, BQ, 2 * DH), bf16),
                    pltpu.VMEM((3 * blocks + 1, DH, BQ), bf16),
                    pltpu.VMEM((3 * blocks + 1, DH, BQ), bf16),
                    pltpu.VMEM((3 * blocks + 1, BQ, DH), f32),
                    pltpu.VMEM((2 * BQ, 2 * DH), bf16),
                    pltpu.VMEM((2 * BQ, 2 * DH), bf16),
                    pltpu.VMEM((keys, 2 * DH), f32),
                    pltpu.VMEM((keys, 2 * DH), bf16),
                    pltpu.VMEM((3 * blocks + 1, BQ, 2 * DH), f32),
                ],
            ),
            out_shape=[
                whole,
                whole,
                jax.ShapeDtypeStruct((parts - 1, 2, blocks, rows, h * DH), bf16),
                jax.ShapeDtypeStruct((blocks, BQ, h * 2 * DH), f32),
                jax.ShapeDtypeStruct((blocks, BQ, h * 2 * DH), bf16),
                jax.ShapeDtypeStruct((blocks, BQ, h * 2 * DH), bf16),
            ],
            input_output_aliases={10 + i: i for i in range(aliased)},
            compiler_params=params(),
            cost_estimate=pl.CostEstimate(
                flops=12 * h * blocks * keys * BQ * DH,
                transcendentals=h * blocks * keys * BQ,
                bytes_accessed=6 * 2**20 * h,
            ),
            name="attend",
        )(meta, *(key_rows, value_rows, query_rows, cotangent), x_in, a_own, b_own, a_in, b_in, *carried)
        outs["att"], outs["dq"] = att, dq
        sends.append((c, h, meta, y_att, kept, near(a_grad, 0), near(b_grad, 1)))

    def return_pieces(y):
        return [exchange(y[s - 1], "head", -s) for s in range(1, parts)]

    returned = []
    for c, h, meta, y_att, kept, a_grad, b_grad in sends:
        back_att = return_pieces(y_att)
        own_spec = pl.BlockSpec((blocks, rows, DH), lambda i, m: (0, 0, m[1] + i))
        wide_spec = pl.BlockSpec((blocks, BQ, 2 * DH), lambda i, m: (0, 0, i))
        piece = pl.BlockSpec((parts - 1, 2, blocks, rows, DH), lambda i, m: (0, 0, 0, 0, i))
        carried = [outs["dk"], outs["dv"]] if "dk" in outs else []
        aliased = len(carried)
        dk, dv, y_grad = pl.pallas_call(
            functools.partial(combine_kernel, blocks=blocks, parts=parts, rows=rows, aliased=aliased),
            grid_spec=pltpu.PrefetchScalarGridSpec(
                num_scalar_prefetch=1,
                grid=(h,),
                in_specs=[wide_spec] * 3 + [pl.BlockSpec(memory_space=pl.ANY)] * aliased,
                out_specs=[own_spec, own_spec, piece],
                scratch_shapes=[pltpu.VMEM((blocks, BQ, 2 * DH), bf16)],
            ),
            out_shape=[
                whole,
                whole,
                jax.ShapeDtypeStruct((parts - 1, 2, blocks, rows, h * DH), bf16),
            ],
            input_output_aliases={4 + i: i for i in range(aliased)},
            compiler_params=params(),
            name="combine",
        )(meta, kept, a_grad, b_grad, *carried)
        outs["dk"], outs["dv"] = dk, dv
        returned.append((c, h, back_att, return_pieces(y_grad)))

    results = {name: outs[name] for name in ("att", "dq", "dk", "dv")}
    for c, h, back_att, back_grad in returned:
        for s in range(1, parts):
            lane = (parts * c + ((here + parts - s) % parts) * h) * DH
            for name, piece in (
                ("att", back_att[s - 1][0]),
                ("dq", back_att[s - 1][1]),
                ("dk", back_grad[s - 1][0]),
                ("dv", back_grad[s - 1][1]),
            ):
                results[name] = lax.dynamic_update_slice_in_dim(results[name], piece, lane, 2)
    return (results["att"], results["dq"], results["dk"], results["dv"])


def solution(mesh):
    rows = P(("groups", "ctx", "sub"), "head", None)
    return jax.shard_map(
        shards,
        mesh=mesh,
        in_specs=(rows, rows, rows, rows, P("groups", None), P("groups")),
        out_specs=(rows, rows, rows, rows),
        check_vma=False,
    )
```
